32 devices in a mesh: rows: 8 (over y, x, core), cols: 4 (over z).
Axes of the slice: x: 2, y: 2, z: 4, core: 2. Of those that a mesh axis runs over, the one named last changes fastest.
Arguments:
- embeddings: bfloat16 [12288, 128], P('rows'), may hold values from -6 to 6
- length_scale: bfloat16 [12288], P('rows'), may hold values from 0.25 to 0.69921875
- start_vectors: float32 [128, 12288], P('cols', 'rows'), may hold values from -6 to 6
- neighbour_ids: int32 [48, 12], P('rows'), may hold values from 0 to 47, as said below
- neighbour_counts: int32 [48], P('rows'), may hold values from 1 to 12
Outputs:
- basis: float32 [128, 12288], P('cols', 'rows')
The draws below stay inside these ranges and needn't reach their ends.
Inputs may be any that keep to these rules, and one draw needn't show every extreme that they name: `neighbour_ids`: slot 0 of a row block names the block itself; the slots from neighbour_counts on repeat the block itself and are unused; the used ids of one block are distinct and name blocks held by the same index of rows or by an index one away along rows.
All inputs are finite; a program needn't handle non-finite values.
Results may differ from the reference program's by a relative error of at most 0.0003.
Values may be sent and summed in bfloat16 or wider, within the bound.
A program may use at most 64 MiB of HBM per device.

```python
import math
import jax
import jax.numpy as jnp
from jax import lax

BS = 256
E = 128
K = 128
MAXNB = 12
ITERS = 3
NB_DEV = 6
NBLK = 48
NPTS = 12288


def neighbour_pattern(key):
    base_key = jax.random.fold_in(key, 4211)
    sub_keys = jax.random.split(base_key, 5)
    devices = NBLK // NB_DEV
    block_ids = jnp.arange(NBLK, dtype=jnp.int32)
    owner_dev = block_ids // NB_DEV
    heavy_dev = jax.random.randint(sub_keys[0], (devices,), 0, 4) == 0
    base_count = jax.random.randint(sub_keys[1], (NBLK,), 1, 5)
    extra_count = jax.random.randint(sub_keys[2], (NBLK,), 0, MAXNB - 3)
    heavy_count = jnp.minimum(base_count + extra_count + 2, MAXNB)
    counts = jnp.where(heavy_dev[owner_dev], heavy_count, base_count)
    counts = jnp.minimum(counts, MAXNB)
    forced_block = jax.random.randint(sub_keys[3], (), 0, NBLK)
    counts = jnp.where(block_ids == forced_block, MAXNB, counts)
    cand_span = 3 * NB_DEV
    cand_off = jnp.arange(cand_span, dtype=jnp.int32)
    candidates = (owner_dev[:, None] - 1) * NB_DEV + cand_off[None, :]
    usable = (candidates >= 0) & (candidates < NBLK) & (candidates != block_ids[:, None])
    scores = jax.random.randint(sub_keys[4], (NBLK, cand_span), 0, 1 << 20)
    rank_key = jnp.where(usable, scores, 1 << 20) * cand_span + cand_off[None, :]
    ordering = jnp.argsort(rank_key, axis=1)
    picked = jnp.take_along_axis(candidates, ordering[:, :MAXNB - 1], axis=1)
    id_table = jnp.concatenate([block_ids[:, None], picked], axis=1)
    slot_pos = jnp.arange(MAXNB, dtype=jnp.int32)
    id_table = jnp.where(slot_pos[None, :] < counts[:, None], id_table, block_ids[:, None])
    return (id_table.astype(jnp.int32), counts.astype(jnp.int32))


def draw_neighbour_ids(key, part):
    id_table, counts = neighbour_pattern(key)
    return id_table


def draw_neighbour_counts(key, part):
    id_table, counts = neighbour_pattern(key)
    return counts


def levels(stream_key, dims, shards, least, high):
    factor_of = 1.0
    for dim, parts in shards:
        steps = jax.random.uniform(jax.random.fold_in(jax.random.fold_in(stream_key, 6), dim), (parts,), jnp.float32, least / len(shards), high / len(shards))
        factor_of = factor_of * jnp.repeat(jnp.exp(steps), dims[dim] // parts).reshape((-1,) + (1,) * (len(dims) - 1 - dim))
    return factor_of


def centred(own_key, extent, spread, reach, cuts=(), held_as=jnp.bfloat16):
    loudness = levels(own_key, extent, cuts, -0.22, 0.18) if cuts else 1.0
    array = jax.random.normal(own_key, extent, jnp.float32) * spread * loudness
    return jnp.minimum(jnp.maximum(array, -reach), reach).astype(held_as)


def setup_inputs(seed: int = 0) -> dict:
    streams_of = jax.random.split(jax.random.key(seed), 6)
    return {
        "embeddings": centred(streams_of[0], (NPTS, E), 1.0, 6.0, ((0, 8),)),
        "length_scale": jnp.clip(jnp.exp(math.log(0.69921875) - 1.0285027 * jax.random.uniform(streams_of[1], (NPTS,), jnp.float32) ** levels(streams_of[1], (NPTS,), ((0, 8),), -0.2, 0.2)), 0.25, 0.69921875).astype(jnp.bfloat16),
        "start_vectors": centred(streams_of[2], (K, NPTS), 1.0, 6.0, ((0, 4), (1, 8)), jnp.float32),
        "neighbour_ids": draw_neighbour_ids(jax.random.fold_in(streams_of[5], 71), 0),
        "neighbour_counts": draw_neighbour_counts(jax.random.fold_in(streams_of[5], 71), 0),
    }


highest = lax.Precision.HIGHEST

def block_tiles(block_id, neighbour_ids, neighbour_counts, blocks_emb, blocks_sq, blocks_bw):
    col_ids = neighbour_ids[block_id]
    row_emb = blocks_emb[block_id].astype(jnp.float32)
    col_emb = blocks_emb[col_ids].astype(jnp.float32)
    inner_prod = jnp.einsum('pe,sqe->spq', row_emb, col_emb)
    distance = blocks_sq[block_id][None, :, None] + blocks_sq[col_ids][:, None, :] - 2.0 * inner_prod
    tile_block = jnp.exp(-distance / (2.0 * E * blocks_bw[block_id][None, :, None] * blocks_bw[col_ids][:, None, :]))
    diagonal_mask = jnp.arange(BS)[:, None] == jnp.arange(BS)[None, :]
    on_self = (col_ids == block_id)[:, None, None] & diagonal_mask[None]
    is_live = (jnp.arange(MAXNB) < neighbour_counts[block_id])[:, None, None]
    tile_block = jnp.where(on_self | jnp.logical_not(is_live), 0.0, tile_block)
    return (tile_block, col_ids)

def reference(embeddings, length_scale, start_vectors, neighbour_ids, neighbour_counts):
    blocks_emb = embeddings.reshape(NBLK, BS, E)
    as_float = embeddings.astype(jnp.float32)
    blocks_sq = lax.optimization_barrier(jnp.sum(as_float * as_float, axis=-1)).reshape(NBLK, BS)
    blocks_bw = length_scale.astype(jnp.float32).reshape(NBLK, BS)
    block_list = jnp.arange(NBLK, dtype=jnp.int32)

    def degree_of(block_id):
        tile_block, col_ids = block_tiles(block_id, neighbour_ids, neighbour_counts, blocks_emb, blocks_sq, blocks_bw)
        return lax.optimization_barrier(jnp.sum(tile_block, axis=(0, 2)))
    degree = lax.map(degree_of, block_list).reshape(NPTS)
    scale = 1.0 / jnp.sqrt(degree)
    iterate = start_vectors
    for iteration in range(ITERS):
        weighted = (iterate * scale[None, :]).reshape(K, NBLK, BS)

        def apply_block(block_id):
            tile_block, col_ids = block_tiles(block_id, neighbour_ids, neighbour_counts, blocks_emb, blocks_sq, blocks_bw)
            return jnp.einsum('ksq,spq->kp', weighted[:, col_ids, :], tile_block, precision=highest)
        product = lax.map(apply_block, block_list).transpose(1, 0, 2).reshape(K, NPTS)
        iterate = 0.5 * (iterate + scale[None, :] * product)
    gram_mat = jnp.dot(iterate, iterate.T, precision=highest) / NPTS
    low_factor = jnp.linalg.cholesky(gram_mat)
    inverse = lax.linalg.triangular_solve(low_factor, jnp.eye(K, dtype=jnp.float32), left_side=True, lower=True)
    return jnp.dot(inverse, iterate, precision=highest)
```

```python
import functools

import jax
import jax.numpy as jnp
from jax import lax
from jax.experimental import pallas as pl
from jax.experimental.pallas import tpu as pltpu
from jax.sharding import PartitionSpec as P

ITERS = 3
GROUP = 4
F32 = jnp.float32
BF16 = jnp.bfloat16
highest = lax.Precision.HIGHEST
VMEM = pl.BlockSpec(memory_space=pltpu.VMEM)
SMEM = pl.BlockSpec(memory_space=pltpu.SMEM)
NT = (((1,), (1,)), ((), ()))


def passed_along(value, axis, steps):
    count = lax.axis_size(axis)
    leading, last = (max(0, -steps), min(count, count - steps))
    return lax.ppermute(value, axis, [(source, source + steps) for source in range(leading, last)])


def split(value):
    high = value.astype(BF16)
    return high, (value - high.astype(F32)).astype(BF16)


def features(emb, left_side):
    size, width = emb.shape
    wide = emb.astype(F32)
    norm = jnp.sum(wide * wide, axis=1, keepdims=True)
    part0 = norm.astype(BF16).astype(F32)
    part1 = (norm - part0).astype(BF16).astype(F32)
    part2 = norm - part0 - part1
    lane = lax.broadcasted_iota(jnp.int32, (size, width), 1)
    base = 3 if left_side else 0
    ones = jnp.where((lane >= 3 - base) & (lane < 6 - base), 1.0, 0.0)
    side = jnp.where(lane == base, -part0, ones)
    side = jnp.where(lane == base + 1, -part1, side)
    side = jnp.where(lane == base + 2, -part2, side)
    main = wide if left_side else 2.0 * wide
    return jnp.concatenate([main.astype(BF16), side.astype(BF16)], axis=1)


def rate_of(spread, width):
    return (1.4426950408889634 / (2.0 * width)) ** 0.5 / spread


def listing(ids, counts, row_here, rows, cols, near):
    blocks, slots = ids.shape
    first = row_here * blocks
    total = jnp.int32(0)
    for b in range(blocks):
        count = counts[b]
        for s in range(slots):
            gap = ids[b, s] - first
            inside = (gap >= 0) & (gap < blocks)
            wanted = inside if near else jnp.logical_not(inside)
            rows[total] = b
            cols[total] = gap if near else jnp.where(gap < 0, gap + blocks, gap)
            total = total + jnp.where(wanted & (s < count), 1, 0)
    for pad in range(GROUP):
        rows[total + pad] = 0
        cols[total + pad] = 0
    return total


def tiles_kernel(near, *refs):
    if near:
        (here, ids, counts, emb, spread, tiles, degree, rows, cols, groups,
         left, left_rate, right) = refs
        far_set = [(emb, spread)]
    else:
        (here, ids, counts, emb, spread, emb_l, spread_l, emb_r, spread_r, near_degree, start,
         tiles, scale, panel, weighted, rows, cols, groups, left, left_rate, right, degree) = refs
        far_set = [(emb_l, spread_l), (emb_r, spread_r)]
    blocks, size, width = emb.shape
    total = listing(ids, counts, here[0], rows, cols, near)
    groups[0] = (total + GROUP - 1) // GROUP
    for b in range(blocks):
        right[b] = features(emb[b], False)
    position = 0
    for far_emb, far_spread in far_set:
        for b in range(blocks):
            left[position] = features(far_emb[b], True)
            rate = rate_of(far_spread[b].astype(F32), width)
            left_rate[position] = jnp.broadcast_to(rate, (128, size)).T
            position += 1
    degree[...] = jnp.zeros(degree.shape, F32) if near else near_degree[...]
    if near:
        apart = lax.broadcasted_iota(jnp.int32, (size, size), 0) != lax.broadcasted_iota(
            jnp.int32, (size, size), 1
        )

    def one(t, carry):
        b, c = rows[t], cols[t]
        gap = lax.dot_general(left[c], right[b], NT, preferred_element_type=F32)
        rate = left_rate[c]
        own = rate_of(spread[b].astype(F32), width)
        tile = jnp.exp2(gap * jnp.concatenate([rate] * (size // 128), axis=1) * own)
        if near:
            tile = jnp.where(apart | (b != c), tile, 0.0)
        degree[b] += jnp.sum(tile, axis=0, keepdims=True)
        high, low = split(tile)
        tiles[t, :size] = high
        tiles[t, size:] = low
        return carry

    lax.fori_loop(0, total, one, 0)
    for pad in range(GROUP - 1):
        tiles[total + pad] = jnp.zeros((2 * size, size), BF16)
    if not near:
        count = start.shape[0]
        for b in range(blocks):
            factor = 1.0 / jnp.sqrt(degree[b])
            scale[b] = factor
            vecs = start[:, b * size:(b + 1) * size]
            panel[b] = vecs
            high, low = split(vecs * factor)
            weighted[b, :count] = high
            weighted[b, count:] = low


def add_products(rows, cols, groups, tiles, vectors, total):
    count, size = total.shape[1:]

    def one(group, carry):
        found = []
        for place in range(GROUP):
            t = group * GROUP + place
            both = vectors[cols[t]]
            out = jnp.dot(both, tiles[t, :size], preferred_element_type=F32)
            more = jnp.dot(both[:count], tiles[t, size:], preferred_element_type=F32)
            found.append((rows[t], out[:count] + out[count:] + more))
        for b, value in found:
            total[b] += value
        return carry

    lax.fori_loop(0, groups[0], one, 0)


def near_product_kernel(rows, cols, groups, tiles, weighted, product):
    product[...] = jnp.zeros(product.shape, F32)
    add_products(rows, cols, groups, tiles, weighted, product)


def far_product_kernel(final, rows, cols, groups, tiles, from_left, from_right, near, scale,
                       panel, *rest):
    if final:
        out, vectors, total = rest
    else:
        out, weighted, vectors, total = rest
    blocks, count, size = panel.shape
    for b in range(blocks):
        vectors[b] = from_left[b]
        vectors[blocks + b] = from_right[b]
    total[...] = near[...]
    add_products(rows, cols, groups, tiles, vectors, total)
    for b in range(blocks):
        factor = scale[b]
        vecs = 0.5 * (panel[b] + factor * total[b])
        if final:
            out[:, b * size:(b + 1) * size] = vecs
        else:
            out[b] = vecs
            high, low = split(vecs * factor)
            weighted[b, :count] = high
            weighted[b, count:] = low


def params():
    return pltpu.CompilerParams(vmem_limit_bytes=20 << 20)


def local(embeddings, length_scale, start_vectors, neighbour_ids, neighbour_counts):
    blocks, slots = neighbour_ids.shape
    points, width = embeddings.shape
    size = points // blocks
    count = start_vectors.shape[0]
    here = lax.axis_index("rows").astype(jnp.int32).reshape(1)
    col_here = lax.axis_index("cols")
    shape = jax.ShapeDtypeStruct
    emb = embeddings.reshape(blocks, size, width)
    spread = length_scale.reshape(blocks, 1, size)
    sides = [passed_along((emb, spread), "rows", step) for step in (1, -1)]
    near_max = blocks * min(slots, blocks) + GROUP
    far_max = blocks * (slots - 1) + GROUP

    def lists(extent):
        return [shape((extent,), jnp.int32), shape((extent,), jnp.int32), shape((1,), jnp.int32)]

    def work(sets):
        return [
            pltpu.VMEM((sets * blocks, size, 2 * width), BF16),
            pltpu.VMEM((sets * blocks, size, 128), F32),
            pltpu.VMEM((blocks, size, 2 * width), BF16),
        ]

    def tile_cost(number):
        return pl.CostEstimate(
            flops=number * size * size * 2 * width * 2, transcendentals=number * size * size,
            bytes_accessed=number * size * size * 4)

    near_tiles, near_degree, near_rows, near_cols, near_groups = pl.pallas_call(
        functools.partial(tiles_kernel, True),
        out_shape=[pltpu.VMEM((near_max, 2 * size, size), BF16), shape((blocks, 1, size), F32)]
        + lists(near_max),
        in_specs=[SMEM] * 3 + [VMEM] * 2,
        out_specs=[VMEM] * 2 + [SMEM] * 3,
        scratch_shapes=work(1),
        compiler_params=params(),
        cost_estimate=tile_cost(20),
        name="near_tiles",
    )(here, neighbour_ids, neighbour_counts, emb, spread)
    block_f32 = shape((blocks, count, size), F32)
    block_both = shape((blocks, 2 * count, size), BF16)
    far_tiles, scale, panel, weighted, far_rows, far_cols, far_groups = pl.pallas_call(
        functools.partial(tiles_kernel, False),
        out_shape=[pltpu.VMEM((far_max, 2 * size, size), BF16), shape((blocks, 1, size), F32),
                   block_f32, block_both] + lists(far_max),
        in_specs=[SMEM] * 3 + [VMEM] * 8,
        out_specs=[VMEM] * 4 + [SMEM] * 3,
        scratch_shapes=work(2) + [pltpu.VMEM((blocks, 1, size), F32)],
        compiler_params=params(),
        cost_estimate=tile_cost(30),
        name="far_tiles",
    )(here, neighbour_ids, neighbour_counts, emb, spread, *sides[0], *sides[1], near_degree,
      start_vectors)

    for iteration in range(ITERS):
        final = iteration == ITERS - 1
        from_left = passed_along(weighted, "rows", 1)
        from_right = passed_along(weighted, "rows", -1)
        near = pl.pallas_call(
            near_product_kernel,
            out_shape=block_f32,
            in_specs=[SMEM] * 3 + [VMEM] * 2,
            out_specs=VMEM,
            compiler_params=params(),
            cost_estimate=tile_cost(20),
            name="near_product",
        )(near_rows, near_cols, near_groups, near_tiles, weighted)
        done = pl.pallas_call(
            functools.partial(far_product_kernel, final),
            out_shape=[shape((count, points), F32)] if final else [block_f32, block_both],
            in_specs=[SMEM] * 3 + [VMEM] * 6,
            out_specs=[VMEM] if final else [VMEM] * 2,
            scratch_shapes=[pltpu.VMEM((2 * blocks, 2 * count, size), BF16),
                            pltpu.VMEM((blocks, count, size), F32)],
            compiler_params=params(),
            cost_estimate=tile_cost(30),
            name="far_product",
        )(far_rows, far_cols, far_groups, far_tiles, from_left, from_right, near, scale, panel)
        if final:
            flat = done[0]
        else:
            panel, weighted = done
    flat_vecs = lax.all_gather(flat, "cols", axis=0, tiled=True)
    columns = flat_vecs.shape[0]
    total_points = points * lax.axis_size("rows")
    gram_mat = lax.psum(jnp.dot(flat_vecs, flat_vecs.T, precision=highest), "rows")
    gram_mat = gram_mat / total_points
    low_factor = jnp.linalg.cholesky(gram_mat)
    inverse = lax.linalg.triangular_solve(
        low_factor, jnp.eye(columns, dtype=F32), left_side=True, lower=True
    )
    rows_mine = lax.dynamic_slice_in_dim(inverse, col_here * count, count, 0)
    return jnp.dot(rows_mine, flat_vecs, precision=highest)


def solution(mesh):
    placed = (P("rows", None), P("rows"), P("cols", "rows"), P("rows", None), P("rows"))
    return jax.shard_map(
        local, mesh=mesh, in_specs=placed, out_specs=P("cols", "rows"), check_vma=False
    )
```

```python
import functools

import jax
import jax.numpy as jnp
from jax import lax
from jax.experimental import pallas as pl
from jax.experimental.pallas import tpu as pltpu
from jax.sharding import PartitionSpec as P

ITERS = 3
GROUP = 4
F32 = jnp.float32
BF16 = jnp.bfloat16
highest = lax.Precision.HIGHEST
MESH = pl.DeviceIdType.MESH
VMEM = pl.BlockSpec(memory_space=pltpu.VMEM)
SMEM = pl.BlockSpec(memory_space=pltpu.SMEM)
NT = (((1,), (1,)), ((), ()))


def split(value):
    high = value.astype(BF16)
    return high, (value - high.astype(F32)).astype(BF16)


def features(emb, left_side):
    size, width = emb.shape
    wide = emb.astype(F32)
    norm = jnp.sum(wide * wide, axis=1, keepdims=True)
    part0 = norm.astype(BF16).astype(F32)
    part1 = (norm - part0).astype(BF16).astype(F32)
    part2 = norm - part0 - part1
    lane = lax.broadcasted_iota(jnp.int32, (size, width), 1)
    base = 3 if left_side else 0
    ones = jnp.where((lane >= 3 - base) & (lane < 6 - base), 1.0, 0.0)
    side = jnp.where(lane == base, -part0, ones)
    side = jnp.where(lane == base + 1, -part1, side)
    side = jnp.where(lane == base + 2, -part2, side)
    main = wide if left_side else 2.0 * wide
    return jnp.concatenate([main.astype(BF16), side.astype(BF16)], axis=1)


def rate_of(spread, width):
    return (1.4426950408889634 / (2.0 * width)) ** 0.5 / spread


def listing(ids, counts, row_here, rows, cols):
    blocks, slots = ids.shape
    first = (row_here - 1) * blocks
    for b in range(blocks):
        rows[b] = b
        cols[b] = blocks + b
    total = jnp.int32(blocks)
    for b in range(blocks):
        count = counts[b]
        for s in range(1, slots):
            rows[total] = b
            cols[total] = ids[b, s] - first
            total = total + jnp.where(s < count, 1, 0)
    for pad in range(GROUP):
        rows[total + pad] = 0
        cols[total + pad] = blocks
    return total


def tiles_kernel(here, ids, counts, emb, spread, emb_l, spread_l, emb_r, spread_r, start,
                 tiles, scale, panel, weighted, rows, cols, groups, left, left_rate, right,
                 right_rate, degree):
    blocks, size, width = emb.shape
    total = listing(ids, counts, here[0], rows, cols)
    groups[0] = (total + GROUP - 1) // GROUP
    position = 0
    for far_emb, far_spread in [(emb_l, spread_l), (emb, spread), (emb_r, spread_r)]:
        for b in range(blocks):
            left[position] = features(far_emb[b], True)
            rate = rate_of(far_spread[b], width)
            left_rate[position] = jnp.broadcast_to(rate, (128, size)).T
            position += 1
    for b in range(blocks):
        right[b] = features(emb[b], False)
        right_rate[b] = rate_of(spread[b], width)

    def tile_of(b, c):
        gap = lax.dot_general(left[c], right[b], NT, preferred_element_type=F32)
        rate = jnp.concatenate([left_rate[c]] * (size // 128), axis=1)
        return jnp.exp2(gap * rate * right_rate[b])

    def keep(t, tile):
        high, low = split(tile)
        tiles[t, :size] = high
        tiles[t, size:] = low
        return jnp.sum(tile, axis=0, keepdims=True)

    apart = lax.broadcasted_iota(jnp.int32, (size, size), 0) != lax.broadcasted_iota(
        jnp.int32, (size, size), 1
    )
    for b in range(blocks):
        degree[b] = keep(b, jnp.where(apart, tile_of(b, blocks + b), 0.0))

    def turn(step, carry):
        first = blocks + 2 * step
        found = []
        for t in (first, first + 1):
            b = rows[t]
            part = keep(t, tile_of(b, cols[t]))
            found.append((b, jnp.where(t < total, part, 0.0)))
        for b, part in found:
            degree[b] += part
        return carry

    lax.fori_loop(0, (total - blocks + 1) // 2, turn, 0)
    for pad in range(GROUP - 1):
        tiles[total + pad] = jnp.zeros((2 * size, size), BF16)
    count = start.shape[0]
    for b in range(blocks):
        factor = 1.0 / jnp.sqrt(degree[b])
        scale[b] = factor
        vecs = start[:, b * size:(b + 1) * size]
        panel[b] = vecs
        high, low = split(vecs * factor)
        weighted[b, :count] = high
        weighted[b, count:] = low


def product_kernel(final, rows, cols, groups, tiles, from_left, own, from_right, scale, panel,
                   *rest):
    if final:
        out, vectors, total = rest
    else:
        out, weighted, vectors, total = rest
    blocks, count, size = panel.shape
    for b in range(blocks):
        vectors[b] = from_left[b]
        vectors[blocks + b] = own[b]
        vectors[2 * blocks + b] = from_right[b]
    total[...] = jnp.zeros(total.shape, F32)

    def one(group, carry):
        found = []
        for place in range(GROUP):
            t = group * GROUP + place
            both = vectors[cols[t]]
            value = jnp.dot(both, tiles[t, :size], preferred_element_type=F32)
            more = jnp.dot(both[:count], tiles[t, size:], preferred_element_type=F32)
            found.append((rows[t], value[:count] + value[count:] + more))
        for b, value in found:
            total[b] += value
        return carry

    lax.fori_loop(0, groups[0], one, 0)
    piece = out.shape[-1]
    for b in range(blocks):
        factor = scale[b]
        vecs = 0.5 * (panel[b] + factor * total[b])
        if final:
            out[:, b * size:(b + 1) * size] = vecs
        else:
            out[b] = vecs
            high, low = split(vecs * factor)
            weighted[b, :count] = high
            weighted[b, count:] = low


def greet(barrier, peers):
    for peer in peers:
        pl.semaphore_signal(barrier, inc=1, device_id=peer, device_id_type=MESH)
    pl.semaphore_wait(barrier, len(peers))


def exchange_kernel(extent, number, *refs):
    values = refs[:number]
    outs = refs[number:3 * number]
    lands = refs[3 * number:5 * number]
    send_sem, recv_sem = refs[5 * number:]
    row, col = lax.axis_index("rows"), lax.axis_index("cols")
    barrier = pltpu.get_barrier_semaphore()
    sides = [(row < extent - 1, row + 1), (row > 0, row - 1)]
    for there, other in sides:
        @pl.when(there)
        def _():
            pl.semaphore_signal(barrier, inc=1, device_id=(other, col), device_id_type=MESH)
    before = jnp.where(row > 0, 1, 0)
    after = jnp.where(row < extent - 1, 1, 0)
    pl.semaphore_wait(barrier, before + after)

    def copy(i, way, other):
        return pltpu.make_async_remote_copy(
            src_ref=values[i], dst_ref=lands[2 * i + way],
            send_sem=send_sem.at[2 * i + way], recv_sem=recv_sem.at[2 * i + way],
            device_id=(other, col), device_id_type=MESH)

    for way, (there, other) in enumerate(sides):
        @pl.when(there)
        def _():
            for i in range(number):
                copy(i, way, other).start()
    for way, (there, other) in enumerate(sides):
        source_there, source = sides[1 - way]

        @pl.when(source_there)
        def _():
            for i in range(number):
                copy(i, way, source).wait_recv()
                outs[2 * i + way][...] = lands[2 * i + way][...]

        @pl.when(jnp.logical_not(source_there))
        def _():
            for i in range(number):
                outs[2 * i + way][...] = jnp.zeros(values[i].shape, values[i].dtype)
    for way, (there, other) in enumerate(sides):
        @pl.when(there)
        def _():
            for i in range(number):
                copy(i, way, other).wait_send()


def exchange(extent, values, collective_id, name):
    number = len(values)
    both = [value for value in values for _ in range(2)]
    return pl.pallas_call(
        functools.partial(exchange_kernel, extent, number),
        out_shape=[jax.ShapeDtypeStruct(v.shape, v.dtype) for v in both],
        in_specs=[VMEM] * number,
        out_specs=[VMEM] * (2 * number),
        scratch_shapes=[pltpu.VMEM(v.shape, v.dtype) for v in both]
        + [pltpu.SemaphoreType.DMA((2 * number,)), pltpu.SemaphoreType.DMA((2 * number,))],
        compiler_params=params(collective_id=collective_id, has_side_effects=True),
        name=name,
    )(*values)


def spread_out(extent, here, at, sources, lands, send_sem, recv_sem):
    copies = []
    for gap in range(1, extent):
        peer = lax.rem(here + gap, extent)
        copies.append(pltpu.make_async_remote_copy(
            src_ref=sources(peer), dst_ref=lands(here), send_sem=send_sem.at[gap - 1],
            recv_sem=recv_sem.at[gap - 1], device_id=at(peer), device_id_type=MESH))
        copies[-1].start()
    for copy in copies:
        copy.wait()


def gram_kernel(row_extent, col_extent, flat, gram_out, turned_out, send, turned, part, part_got,
                block, block_got, whole, last, *sems):
    row, col = lax.axis_index("rows"), lax.axis_index("cols")
    count, points = flat.shape
    piece = points // col_extent
    columns = count * col_extent

    def along_cols(peer):
        return (row, peer)

    def along_rows(peer):
        return (peer, col)

    greet(pltpu.get_barrier_semaphore(),
          [along_cols(lax.rem(col + gap, col_extent)) for gap in range(1, col_extent)]
          + [along_rows(lax.rem(row + gap, row_extent)) for gap in range(1, row_extent)])
    for peer in range(col_extent):
        send[peer] = flat[:, peer * piece:(peer + 1) * piece]
    spread_out(col_extent, col, along_cols, lambda peer: send.at[peer],
               lambda me: turned.at[me], sems[0], sems[1])
    turned[col] = send[col]
    vecs = turned[...].reshape(columns, piece)
    turned_out[...] = vecs
    part[...] = lax.dot_general(
        vecs, vecs, NT, precision=highest, preferred_element_type=F32
    ).reshape(part.shape)
    spread_out(col_extent, col, along_cols, lambda peer: part.at[peer],
               lambda me: part_got.at[me], sems[2], sems[3])
    part_got[col] = part[col]
    block[...] = sum(part_got[peer] for peer in range(col_extent))
    spread_out(row_extent, row, along_rows, lambda peer: block,
               lambda me: block_got.at[me], sems[4], sems[5])
    block_got[row] = block[...]
    last[...] = sum(block_got[peer] for peer in range(row_extent)) / (points * row_extent)
    spread_out(col_extent, col, along_cols, lambda peer: last,
               lambda me: whole.at[me], sems[6], sems[7])
    whole[col] = last[...]
    gram_out[...] = whole[...].reshape(columns, columns)


def inverse_factor(matrix):
    side = matrix.shape[0]
    count = side // 8
    shape = (8, side)
    lane = lax.broadcasted_iota(jnp.int32, shape, 1)
    sub = lax.broadcasted_iota(jnp.int32, shape, 0)
    left = [matrix[8 * g:8 * g + 8] for g in range(count)]
    right = [jnp.where(lane == sub + 8 * g, 1.0, 0.0) for g in range(count)]

    def spread_column(value, j):
        return jnp.broadcast_to(value[:, j:j + 1], shape)

    def spread_row(value, i):
        return jnp.broadcast_to(value[i:i + 1], shape)

    out = []
    for g in range(count):
        first = 8 * g
        column = [spread_column(left[g], first + k) for k in range(8)]
        entry = {(i, k): spread_row(column[k], i) for k in range(8) for i in range(k, 8)}
        inv, mult = [], {}
        for k in range(8):
            inv.append(1.0 / entry[k, k])
            for i in range(k + 1, 8):
                mult[i, k] = entry[i, k] * inv[k]
            for l in range(k + 1, 8):
                for i in range(l, 8):
                    entry[i, l] = entry[i, l] - mult[i, k] * entry[l, k]
        rows = []
        for i in range(8):
            a, w = spread_row(left[g], i), spread_row(right[g], i)
            for k in range(i):
                a = a - mult[i, k] * rows[k][0]
                w = w - mult[i, k] * rows[k][1]
            rows.append((a, w))
        done = jnp.zeros(shape, F32)
        for i in range(8):
            done = jnp.where(sub == i, rows[i][1] * (1.0 / jnp.sqrt(entry[i, i])), done)
        out.append(done)
        solved = [None] * 8
        for i in reversed(range(8)):
            a, w = rows[i][0] * inv[i], rows[i][1] * inv[i]
            for k in range(i + 1, 8):
                a = a - mult[k, i] * solved[k][0]
                w = w - mult[k, i] * solved[k][1]
            solved[i] = (a, w)
        for h in range(g + 1, count):
            a, w = left[h], right[h]
            for k in range(8):
                factor = spread_column(left[h], first + k)
                a = a - factor * solved[k][0]
                w = w - factor * solved[k][1]
            left[h], right[h] = a, w
    return jnp.concatenate(out, axis=0)


def basis_kernel(gram, turned, basis):
    inverse = inverse_factor(gram[...])
    basis[...] = jnp.dot(
        inverse, turned[...], precision=highest, preferred_element_type=F32
    ).reshape(basis.shape)


def return_kernel(col_extent, basis, out, land, send_sem, recv_sem):
    row, col = lax.axis_index("rows"), lax.axis_index("cols")
    piece = basis.shape[-1]

    def along_cols(peer):
        return (row, peer)

    greet(pltpu.get_barrier_semaphore(),
          [along_cols(lax.rem(col + gap, col_extent)) for gap in range(1, col_extent)])
    spread_out(col_extent, col, along_cols, lambda peer: basis.at[peer],
               lambda me: land.at[me], send_sem, recv_sem)
    land[col] = basis[col]
    for peer in range(col_extent):
        out[:, peer * piece:(peer + 1) * piece] = land[peer]


def params(**others):
    return pltpu.CompilerParams(vmem_limit_bytes=12 << 20, **others)


def local(row_extent, col_extent, embeddings, length_scale, start_vectors, neighbour_ids,
          neighbour_counts):
    blocks, slots = neighbour_ids.shape
    points, width = embeddings.shape
    size = points // blocks
    count = start_vectors.shape[0]
    here = lax.axis_index("rows").astype(jnp.int32).reshape(1)
    shape = jax.ShapeDtypeStruct
    dma = pltpu.SemaphoreType.DMA
    emb = embeddings.reshape(blocks, size, width)
    spread = length_scale.astype(F32).reshape(blocks, 1, size)
    emb_l, emb_r, spread_l, spread_r = exchange(row_extent, (emb, spread), 0, "points_exchange")
    most = blocks * slots + GROUP
    block_f32 = shape((blocks, count, size), F32)
    block_both = shape((blocks, 2 * count, size), BF16)
    tiles, scale, panel, weighted, rows, cols, groups = pl.pallas_call(
        tiles_kernel,
        out_shape=[pltpu.VMEM((most, 2 * size, size), BF16), shape((blocks, 1, size), F32),
                   block_f32, block_both, shape((most,), jnp.int32), shape((most,), jnp.int32),
                   shape((1,), jnp.int32)],
        in_specs=[SMEM] * 3 + [VMEM] * 7,
        out_specs=[VMEM] * 4 + [SMEM] * 3,
        scratch_shapes=[
            pltpu.VMEM((3 * blocks, size, 2 * width), BF16),
            pltpu.VMEM((3 * blocks, size, 128), F32),
            pltpu.VMEM((blocks, size, 2 * width), BF16),
            pltpu.VMEM((blocks, 1, size), F32),
            pltpu.VMEM((blocks, 1, size), F32),
        ],
        compiler_params=params(),
        name="tiles",
    )(here, neighbour_ids, neighbour_counts, emb, spread, emb_l, spread_l, emb_r, spread_r,
      start_vectors)

    for iteration in range(ITERS):
        final = iteration == ITERS - 1
        from_left, from_right = exchange(row_extent, (weighted,), 1, "vectors_exchange")
        done = pl.pallas_call(
            functools.partial(product_kernel, final),
            out_shape=[shape((count, points), F32)] if final else [block_f32, block_both],
            in_specs=[SMEM] * 3 + [VMEM] * 6,
            out_specs=[VMEM] if final else [VMEM] * 2,
            scratch_shapes=[pltpu.VMEM((3 * blocks, 2 * count, size), BF16),
                            pltpu.VMEM((blocks, count, size), F32)],
            compiler_params=params(),
            name="product",
        )(rows, cols, groups, tiles, from_left, weighted, from_right, scale, panel)
        if final:
            flat = done[0]
        else:
            panel, weighted = done

    columns = count * col_extent
    piece = points // col_extent
    pieces = pltpu.VMEM((col_extent, count, piece), F32)
    part = pltpu.VMEM((col_extent, count, columns), F32)
    gram, turned = pl.pallas_call(
        functools.partial(gram_kernel, row_extent, col_extent),
        out_shape=[shape((columns, columns), F32), shape((columns, piece), F32)],
        in_specs=[VMEM],
        out_specs=[VMEM] * 2,
        scratch_shapes=[pieces, pieces, part, part, pltpu.VMEM((count, columns), F32),
                        pltpu.VMEM((row_extent, count, columns), F32), part,
                        pltpu.VMEM((count, columns), F32)]
        + [dma((extent - 1,)) for extent in (col_extent, col_extent, row_extent, col_extent)
           for _ in range(2)],
        compiler_params=params(collective_id=2, has_side_effects=True),
        name="gram",
    )(flat)
    basis = pl.pallas_call(
        basis_kernel,
        out_shape=shape((col_extent, count, piece), F32),
        in_specs=[VMEM] * 2,
        out_specs=VMEM,
        compiler_params=params(),
        name="basis",
    )(gram, turned)
    return pl.pallas_call(
        functools.partial(return_kernel, col_extent),
        out_shape=shape((count, points), F32),
        in_specs=[VMEM],
        out_specs=VMEM,
        scratch_shapes=[pieces, dma((col_extent - 1,)), dma((col_extent - 1,))],
        compiler_params=params(collective_id=3, has_side_effects=True),
        name="basis_return",
    )(basis)


def solution(mesh):
    placed = (P("rows", None), P("rows"), P("cols", "rows"), P("rows", None), P("rows"))
    body = functools.partial(local, mesh.shape["rows"], mesh.shape["cols"])
    return jax.shard_map(
        body, mesh=mesh, in_specs=placed, out_specs=P("cols", "rows"), check_vma=False
    )
```

```python
import functools

import jax
import jax.numpy as jnp
from jax import lax
from jax.experimental import pallas as pl
from jax.experimental.pallas import tpu as pltpu
from jax.sharding import PartitionSpec as P

ITERS = 3
GROUP = 4
F32 = jnp.float32
BF16 = jnp.bfloat16
highest = lax.Precision.HIGHEST
MESH = pl.DeviceIdType.MESH
VMEM = pl.BlockSpec(memory_space=pltpu.VMEM)
SMEM = pl.BlockSpec(memory_space=pltpu.SMEM)
HBM = pl.BlockSpec(memory_space=pltpu.HBM)
NT = (((1,), (1,)), ((), ()))


def split(value):
    high = value.astype(BF16)
    return high, (value - high.astype(F32)).astype(BF16)


def features(emb, left_side):
    size, width = emb.shape
    wide = emb.astype(F32)
    norm = jnp.sum(wide * wide, axis=1, keepdims=True)
    part0 = norm.astype(BF16).astype(F32)
    part1 = (norm - part0).astype(BF16).astype(F32)
    part2 = norm - part0 - part1
    lane = lax.broadcasted_iota(jnp.int32, (size, width), 1)
    base = 3 if left_side else 0
    ones = jnp.where((lane >= 3 - base) & (lane < 6 - base), 1.0, 0.0)
    side = jnp.where(lane == base, -part0, ones)
    side = jnp.where(lane == base + 1, -part1, side)
    side = jnp.where(lane == base + 2, -part2, side)
    main = wide if left_side else 2.0 * wide
    return jnp.concatenate([main.astype(BF16), side.astype(BF16)], axis=1)


def rate_of(spread, width):
    return (1.4426950408889634 / (2.0 * width)) ** 0.5 / spread


def listing(ids, counts, row_here, rows, cols):
    blocks, slots = ids.shape
    first = (row_here - 1) * blocks
    for b in range(blocks):
        rows[b] = b
        cols[b] = blocks + b
    total = jnp.int32(blocks)
    for b in range(blocks):
        count = counts[b]
        for s in range(1, slots):
            rows[total] = b
            cols[total] = ids[b, s] - first
            total = total + jnp.where(s < count, 1, 0)
    for pad in range(GROUP):
        rows[total + pad] = 0
        cols[total + pad] = blocks
    return total


def tiles_kernel(ids_there, counts_there, emb, spread, start_there,
                 tiles, scale, panel, weighted, rows, cols, groups, left, left_rate, right,
                 right_rate, degree, ids, counts, start, sem):
    band, size, width = emb.shape
    blocks = band // 3
    copies = [
        pltpu.make_async_copy(source, target, sem.at[i])
        for i, (source, target) in enumerate(
            [(ids_there, ids), (counts_there, counts), (start_there, start)])
    ]
    for copy in copies:
        copy.start()
    copies[0].wait()
    copies[1].wait()
    total = listing(ids, counts, lax.axis_index("rows"), rows, cols)
    groups[0] = (total + GROUP - 1) // GROUP
    for c in range(band):
        left[c] = features(emb[c], True)
        left_rate[c] = jnp.broadcast_to(rate_of(spread[c], width), (128, size)).T
    for b in range(blocks):
        right[b] = features(emb[blocks + b], False)
        right_rate[b] = rate_of(spread[blocks + b], width)

    def tile_of(b, c):
        gap = lax.dot_general(left[c], right[b], NT, preferred_element_type=F32)
        rate = jnp.concatenate([left_rate[c]] * (size // 128), axis=1)
        return jnp.exp2(gap * rate * right_rate[b])

    def keep(t, tile):
        high, low = split(tile)
        tiles[t, :size] = high
        tiles[t, size:] = low
        return jnp.sum(tile, axis=0, keepdims=True)

    apart = lax.broadcasted_iota(jnp.int32, (size, size), 0) != lax.broadcasted_iota(
        jnp.int32, (size, size), 1
    )
    for b in range(blocks):
        degree[b] = keep(b, jnp.where(apart, tile_of(b, blocks + b), 0.0))

    def turn(step, carry):
        first = blocks + GROUP * step
        found = []
        for t in [first + place for place in range(GROUP)]:
            b = rows[t]
            part = keep(t, tile_of(b, cols[t]))
            found.append((b, jnp.where(t < total, part, 0.0)))
        for b, part in found:
            degree[b] += part
        return carry

    lax.fori_loop(0, (total - blocks + GROUP - 1) // GROUP, turn, 0)
    for pad in range(GROUP - 1):
        tiles[total + pad] = jnp.zeros((2 * size, size), BF16)
    copies[2].wait()
    count = start.shape[0]
    for b in range(blocks):
        factor = 1.0 / jnp.sqrt(degree[b])
        scale[b] = factor
        vecs = start[:, b * size:(b + 1) * size]
        panel[b] = vecs
        high, low = split(vecs * factor)
        weighted[b, :count] = high
        weighted[b, count:] = low


def product_kernel(final, rows, cols, groups, tiles, vectors, scale, panel, *rest):
    if final:
        out, total = rest
    else:
        out, weighted, total = rest
    blocks, count, size = panel.shape
    total[...] = jnp.zeros(total.shape, F32)

    def one(group, carry):
        found = []
        for place in range(GROUP):
            t = group * GROUP + place
            both = vectors[cols[t]]
            value = jnp.dot(both, tiles[t, :size], preferred_element_type=F32)
            more = jnp.dot(both[:count], tiles[t, size:], preferred_element_type=F32)
            found.append((rows[t], value[:count] + value[count:] + more))
        for b, value in found:
            total[b] += value
        return carry

    lax.fori_loop(0, groups[0], one, 0)
    for b in range(blocks):
        factor = scale[b]
        vecs = 0.5 * (panel[b] + factor * total[b])
        if final:
            out[:, b * size:(b + 1) * size] = vecs
        else:
            out[b] = vecs
            high, low = split(vecs * factor)
            weighted[b, :count] = high
            weighted[b, count:] = low


def greet(barrier, peers):
    for peer in peers:
        pl.semaphore_signal(barrier, inc=1, device_id=peer, device_id_type=MESH)
    pl.semaphore_wait(barrier, len(peers))


def exchange_kernel(extent, number, *refs):
    values = refs[:number]
    outs = refs[number:2 * number]
    send_sem, recv_sem, own_sem = refs[2 * number:]
    row, col = lax.axis_index("rows"), lax.axis_index("cols")
    barrier = pltpu.get_barrier_semaphore()
    sides = [(row < extent - 1, row + 1), (row > 0, row - 1)]
    for there, other in sides:
        @pl.when(there)
        def _():
            pl.semaphore_signal(barrier, inc=1, device_id=(other, col), device_id_type=MESH)
    before = jnp.where(row > 0, 1, 0)
    after = jnp.where(row < extent - 1, 1, 0)
    pl.semaphore_wait(barrier, before + after)

    def part(i, place):
        blocks = values[i].shape[0]
        return outs[i].at[place * blocks:(place + 1) * blocks]

    def copy(i, way, other):
        return pltpu.make_async_remote_copy(
            src_ref=values[i], dst_ref=part(i, 2 * way),
            send_sem=send_sem.at[2 * i + way], recv_sem=recv_sem.at[2 * i + way],
            device_id=(other, col), device_id_type=MESH)

    for way, (there, other) in enumerate(sides):
        @pl.when(there)
        def _():
            for i in range(number):
                copy(i, way, other).start()
    own = [pltpu.make_async_copy(values[i], part(i, 1), own_sem.at[i]) for i in range(number)]
    for copying in own:
        copying.start()
    for way, (there, other) in enumerate(sides):
        source_there, source = sides[1 - way]

        @pl.when(source_there)
        def _():
            for i in range(number):
                copy(i, way, source).wait_recv()

        @pl.when(jnp.logical_not(source_there))
        def _():
            for i in range(number):
                part(i, 2 * way)[...] = jnp.zeros(values[i].shape, values[i].dtype)
    for way, (there, other) in enumerate(sides):
        @pl.when(there)
        def _():
            for i in range(number):
                copy(i, way, other).wait_send()
    for copying in own:
        copying.wait()


def exchange(extent, values, specs, collective_id, name):
    number = len(values)
    return pl.pallas_call(
        functools.partial(exchange_kernel, extent, number),
        out_shape=[jax.ShapeDtypeStruct((3 * v.shape[0],) + v.shape[1:], v.dtype)
                   for v in values],
        in_specs=specs,
        out_specs=[VMEM] * number,
        scratch_shapes=[pltpu.SemaphoreType.DMA((2 * number,)),
                        pltpu.SemaphoreType.DMA((2 * number,)),
                        pltpu.SemaphoreType.DMA((number,))],
        compiler_params=params(collective_id=collective_id, has_side_effects=True),
        cost_estimate=pl.CostEstimate(flops=0, transcendentals=0, bytes_accessed=16 << 20),
        name=name,
    )(*values)


def spread_out(extent, here, at, sources, lands, send_sem, recv_sem):
    copies = []
    for gap in range(1, extent):
        peer = lax.rem(here + gap, extent)
        copies.append(pltpu.make_async_remote_copy(
            src_ref=sources(peer), dst_ref=lands(here), send_sem=send_sem.at[gap - 1],
            recv_sem=recv_sem.at[gap - 1], device_id=at(peer), device_id_type=MESH))
        copies[-1].start()
    for copy in copies:
        copy.wait()


def gram_kernel(row_extent, col_extent, flat, gram_out, turned_out, send, turned, part, part_got,
                block, block_got, whole, last, *sems):
    row, col = lax.axis_index("rows"), lax.axis_index("cols")
    count, points = flat.shape
    piece = points // col_extent
    columns = count * col_extent

    def along_cols(peer):
        return (row, peer)

    def along_rows(peer):
        return (peer, col)

    greet(pltpu.get_barrier_semaphore(),
          [along_cols(lax.rem(col + gap, col_extent)) for gap in range(1, col_extent)]
          + [along_rows(lax.rem(row + gap, row_extent)) for gap in range(1, row_extent)])
    for peer in range(col_extent):
        send[peer] = flat[:, peer * piece:(peer + 1) * piece]
    spread_out(col_extent, col, along_cols, lambda peer: send.at[peer],
               lambda me: turned.at[me], sems[0], sems[1])
    turned[col] = send[col]
    vecs = turned[...].reshape(columns, piece)
    turned_out[...] = vecs
    part[...] = lax.dot_general(
        vecs, vecs, NT, precision=highest, preferred_element_type=F32
    ).reshape(part.shape)
    spread_out(col_extent, col, along_cols, lambda peer: part.at[peer],
               lambda me: part_got.at[me], sems[2], sems[3])
    part_got[col] = part[col]
    block[...] = sum(part_got[peer] for peer in range(col_extent))
    spread_out(row_extent, row, along_rows, lambda peer: block,
               lambda me: block_got.at[me], sems[4], sems[5])
    block_got[row] = block[...]
    last[...] = sum(block_got[peer] for peer in range(row_extent)) / (points * row_extent)
    spread_out(col_extent, col, along_cols, lambda peer: last,
               lambda me: whole.at[me], sems[6], sems[7])
    whole[col] = last[...]
    gram_out[...] = whole[...].reshape(columns, columns)


def inverse_factor(matrix):
    side = matrix.shape[0]
    count = side // 8
    shape = (8, side)
    lane = lax.broadcasted_iota(jnp.int32, shape, 1)
    sub = lax.broadcasted_iota(jnp.int32, shape, 0)
    left = [matrix[8 * g:8 * g + 8] for g in range(count)]
    right = [jnp.where(lane == sub + 8 * g, 1.0, 0.0) for g in range(count)]

    def spread_column(value, j):
        return jnp.broadcast_to(value[:, j:j + 1], shape)

    def spread_row(value, i):
        return jnp.broadcast_to(value[i:i + 1], shape)

    out = []
    for g in range(count):
        first = 8 * g
        column = [spread_column(left[g], first + k) for k in range(8)]
        entry = {(i, k): spread_row(column[k], i) for k in range(8) for i in range(k, 8)}
        inv, mult = [], {}
        for k in range(8):
            inv.append(1.0 / entry[k, k])
            for i in range(k + 1, 8):
                mult[i, k] = entry[i, k] * inv[k]
            for l in range(k + 1, 8):
                for i in range(l, 8):
                    entry[i, l] = entry[i, l] - mult[i, k] * entry[l, k]
        rows = []
        for i in range(8):
            a, w = spread_row(left[g], i), spread_row(right[g], i)
            for k in range(i):
                a = a - mult[i, k] * rows[k][0]
                w = w - mult[i, k] * rows[k][1]
            rows.append((a, w))
        done = jnp.zeros(shape, F32)
        for i in range(8):
            done = jnp.where(sub == i, rows[i][1] * (1.0 / jnp.sqrt(entry[i, i])), done)
        out.append(done)
        solved = [None] * 8
        for i in reversed(range(8)):
            a, w = rows[i][0] * inv[i], rows[i][1] * inv[i]
            for k in range(i + 1, 8):
                a = a - mult[k, i] * solved[k][0]
                w = w - mult[k, i] * solved[k][1]
            solved[i] = (a, w)
        for h in range(g + 1, count):
            a, w = left[h], right[h]
            for k in range(8):
                factor = spread_column(left[h], first + k)
                a = a - factor * solved[k][0]
                w = w - factor * solved[k][1]
            left[h], right[h] = a, w
    return jnp.concatenate(out, axis=0)


def basis_kernel(gram, turned, basis):
    inverse = inverse_factor(gram[...])
    basis[...] = jnp.dot(
        inverse, turned[...], precision=highest, preferred_element_type=F32
    ).reshape(basis.shape)


def return_kernel(col_extent, basis, out, land, send_sem, recv_sem):
    row, col = lax.axis_index("rows"), lax.axis_index("cols")
    piece = basis.shape[-1]

    def along_cols(peer):
        return (row, peer)

    greet(pltpu.get_barrier_semaphore(),
          [along_cols(lax.rem(col + gap, col_extent)) for gap in range(1, col_extent)])
    spread_out(col_extent, col, along_cols, lambda peer: basis.at[peer],
               lambda me: land.at[me], send_sem, recv_sem)
    land[col] = basis[col]
    for peer in range(col_extent):
        out[:, peer * piece:(peer + 1) * piece] = land[peer]


def held(value):
    return pltpu.with_memory_space_constraint(value, pltpu.HBM)


def params(**others):
    return pltpu.CompilerParams(vmem_limit_bytes=12 << 20, **others)


def local(row_extent, col_extent, embeddings, length_scale, start_vectors, neighbour_ids,
          neighbour_counts):
    blocks, slots = neighbour_ids.shape
    points, width = embeddings.shape
    size = points // blocks
    count = start_vectors.shape[0]
    shape = jax.ShapeDtypeStruct
    dma = pltpu.SemaphoreType.DMA
    emb = embeddings.reshape(blocks, size, width)
    spread = length_scale.astype(F32).reshape(blocks, 1, size)
    band_emb, band_spread = exchange(row_extent, (held(emb), spread), [HBM, VMEM], 0, "points_exchange")
    most = blocks * slots + GROUP
    block_f32 = shape((blocks, count, size), F32)
    block_both = shape((blocks, 2 * count, size), BF16)
    tiles, scale, panel, weighted, rows, cols, groups = pl.pallas_call(
        tiles_kernel,
        out_shape=[pltpu.VMEM((most, 2 * size, size), BF16), shape((blocks, 1, size), F32),
                   block_f32, block_both, shape((most,), jnp.int32), shape((most,), jnp.int32),
                   shape((1,), jnp.int32)],
        in_specs=[HBM] * 2 + [VMEM] * 2 + [HBM],
        out_specs=[VMEM] * 4 + [SMEM] * 3,
        scratch_shapes=[
            pltpu.VMEM((3 * blocks, size, 2 * width), BF16),
            pltpu.VMEM((3 * blocks, size, 128), F32),
            pltpu.VMEM((blocks, size, 2 * width), BF16),
            pltpu.VMEM((blocks, 1, size), F32),
            pltpu.VMEM((blocks, 1, size), F32),
            pltpu.SMEM((blocks, slots), jnp.int32),
            pltpu.SMEM((blocks,), jnp.int32),
            pltpu.VMEM((count, points), F32),
            dma((3,)),
        ],
        compiler_params=params(),
        name="tiles",
    )(held(neighbour_ids), held(neighbour_counts), band_emb, band_spread, held(start_vectors))

    for iteration in range(ITERS):
        final = iteration == ITERS - 1
        (vectors,) = exchange(row_extent, (weighted,), [VMEM], 1, "vectors_exchange")
        done = pl.pallas_call(
            functools.partial(product_kernel, final),
            out_shape=[shape((count, points), F32)] if final else [block_f32, block_both],
            in_specs=[SMEM] * 3 + [VMEM] * 4,
            out_specs=[VMEM] if final else [VMEM] * 2,
            scratch_shapes=[pltpu.VMEM((blocks, count, size), F32)],
            compiler_params=params(),
            name="product",
        )(rows, cols, groups, tiles, vectors, scale, panel)
        if final:
            flat = done[0]
        else:
            panel, weighted = done

    columns = count * col_extent
    piece = points // col_extent
    pieces = pltpu.VMEM((col_extent, count, piece), F32)
    part = pltpu.VMEM((col_extent, count, columns), F32)
    gram, turned = pl.pallas_call(
        functools.partial(gram_kernel, row_extent, col_extent),
        out_shape=[shape((columns, columns), F32), shape((columns, piece), F32)],
        in_specs=[VMEM],
        out_specs=[VMEM] * 2,
        scratch_shapes=[pieces, pieces, part, part, pltpu.VMEM((count, columns), F32),
                        pltpu.VMEM((row_extent, count, columns), F32), part,
                        pltpu.VMEM((count, columns), F32)]
        + [dma((extent - 1,)) for extent in (col_extent, col_extent, row_extent, col_extent)
           for _ in range(2)],
        compiler_params=params(collective_id=2, has_side_effects=True),
        name="gram",
    )(flat)
    basis = pl.pallas_call(
        basis_kernel,
        out_shape=shape((col_extent, count, piece), F32),
        in_specs=[VMEM] * 2,
        out_specs=VMEM,
        compiler_params=params(),
        name="basis",
    )(gram, turned)
    return pl.pallas_call(
        functools.partial(return_kernel, col_extent),
        out_shape=shape((count, points), F32),
        in_specs=[VMEM],
        out_specs=VMEM,
        scratch_shapes=[pieces, dma((col_extent - 1,)), dma((col_extent - 1,))],
        compiler_params=params(collective_id=3, has_side_effects=True),
        name="basis_return",
    )(basis)


def solution(mesh):
    placed = (P("rows", None), P("rows"), P("cols", "rows"), P("rows", None), P("rows"))
    body = functools.partial(local, mesh.shape["rows"], mesh.shape["cols"])
    return jax.shard_map(
        body, mesh=mesh, in_specs=placed, out_specs=P("cols", "rows"), check_vma=False
    )
```

```python
import functools

import jax
import jax.numpy as jnp
from jax import lax
from jax.experimental import pallas as pl
from jax.experimental.pallas import tpu as pltpu
from jax.sharding import PartitionSpec as P

ITERS = 3
GROUP = 4
CHUNKS = 3
F32 = jnp.float32
BF16 = jnp.bfloat16
highest = lax.Precision.HIGHEST
MESH = pl.DeviceIdType.MESH
VMEM = pl.BlockSpec(memory_space=pltpu.VMEM)
SMEM = pl.BlockSpec(memory_space=pltpu.SMEM)
HBM = pl.BlockSpec(memory_space=pltpu.HBM)
NT = (((1,), (1,)), ((), ()))


def split(value):
    high = value.astype(BF16)
    return high, (value - high.astype(F32)).astype(BF16)


def features(emb, left_side):
    size, width = emb.shape
    wide = emb.astype(F32)
    norm = jnp.sum(wide * wide, axis=1, keepdims=True)
    part0 = norm.astype(BF16).astype(F32)
    part1 = (norm - part0).astype(BF16).astype(F32)
    part2 = norm - part0 - part1
    lane = lax.broadcasted_iota(jnp.int32, (size, width), 1)
    base = 3 if left_side else 0
    ones = jnp.where((lane >= 3 - base) & (lane < 6 - base), 1.0, 0.0)
    side = jnp.where(lane == base, -part0, ones)
    side = jnp.where(lane == base + 1, -part1, side)
    side = jnp.where(lane == base + 2, -part2, side)
    main = wide if left_side else 2.0 * wide
    return jnp.concatenate([main.astype(BF16), side.astype(BF16)], axis=1)


def rate_of(spread, width):
    return (1.4426950408889634 / (2.0 * width)) ** 0.5 / spread


def listing(ids, counts, row_here, rows, cols):
    blocks, slots = ids.shape
    first = (row_here - 1) * blocks
    for b in range(blocks):
        rows[b] = b
        cols[b] = blocks + b
    total = jnp.int32(blocks)
    for b in range(blocks):
        count = counts[b]
        for s in range(1, slots):
            rows[total] = b
            cols[total] = ids[b, s] - first
            total = total + jnp.where(s < count, 1, 0)
    for pad in range(GROUP):
        rows[total + pad] = 0
        cols[total + pad] = blocks
    return total


def tiles_kernel(ids_there, counts_there, emb, spread, start_there,
                 tiles, scale, panel, weighted, rows, cols, groups, left, left_rate, right,
                 right_rate, degree, ids, counts, start, sem):
    band, size, width = emb.shape
    blocks = band // 3
    copies = [
        pltpu.make_async_copy(source, target, sem.at[i])
        for i, (source, target) in enumerate(
            [(ids_there, ids), (counts_there, counts), (start_there, start)])
    ]
    for copy in copies:
        copy.start()
    copies[0].wait()
    copies[1].wait()
    total = listing(ids, counts, lax.axis_index("rows"), rows, cols)
    groups[0] = (total + GROUP - 1) // GROUP
    for c in range(band):
        left[c] = features(emb[c], True)
        left_rate[c] = jnp.broadcast_to(rate_of(spread[c], width), (128, size)).T
    for b in range(blocks):
        right[b] = features(emb[blocks + b], False)
        right_rate[b] = rate_of(spread[blocks + b], width)

    def tile_of(b, c):
        gap = lax.dot_general(left[c], right[b], NT, preferred_element_type=F32)
        rate = jnp.concatenate([left_rate[c]] * (size // 128), axis=1)
        return jnp.exp2(gap * rate * right_rate[b])

    def keep(t, tile):
        high, low = split(tile)
        tiles[t, :size] = high
        tiles[t, size:] = low
        return jnp.sum(tile, axis=0, keepdims=True)

    apart = lax.broadcasted_iota(jnp.int32, (size, size), 0) != lax.broadcasted_iota(
        jnp.int32, (size, size), 1
    )
    for b in range(blocks):
        degree[b] = keep(b, jnp.where(apart, tile_of(b, blocks + b), 0.0))

    def turn(step, carry):
        first = blocks + GROUP * step
        found = []
        for t in [first + place for place in range(GROUP)]:
            b = rows[t]
            part = keep(t, tile_of(b, cols[t]))
            found.append((b, jnp.where(t < total, part, 0.0)))
        for b, part in found:
            degree[b] += part
        return carry

    lax.fori_loop(0, (total - blocks + GROUP - 1) // GROUP, turn, 0)
    for pad in range(GROUP - 1):
        tiles[total + pad] = jnp.zeros((2 * size, size), BF16)
    copies[2].wait()
    count = start.shape[0]
    for b in range(blocks):
        factor = 1.0 / jnp.sqrt(degree[b])
        scale[b] = factor
        vecs = start[:, b * size:(b + 1) * size]
        panel[b] = vecs
        high, low = split(vecs * factor)
        weighted[b, :count] = high
        weighted[b, count:] = low


def product_kernel(final, rows, cols, groups, tiles, vectors, scale, panel, *rest):
    if final:
        out, total = rest
    else:
        out, weighted, total = rest
    blocks, count, size = panel.shape
    total[...] = jnp.zeros(total.shape, F32)

    def one(group, carry):
        found = []
        for place in range(GROUP):
            t = group * GROUP + place
            both = vectors[cols[t]]
            value = jnp.dot(both, tiles[t, :size], preferred_element_type=F32)
            more = jnp.dot(both[:count], tiles[t, size:], preferred_element_type=F32)
            found.append((rows[t], value[:count] + value[count:] + more))
        for b, value in found:
            total[b] += value
        return carry

    lax.fori_loop(0, groups[0], one, 0)
    for b in range(blocks):
        factor = scale[b]
        vecs = 0.5 * (panel[b] + factor * total[b])
        if final:
            out[:, b * size:(b + 1) * size] = vecs
        else:
            out[b] = vecs
            high, low = split(vecs * factor)
            weighted[b, :count] = high
            weighted[b, count:] = low


def greet(barrier, peers):
    for peer in peers:
        pl.semaphore_signal(barrier, inc=1, device_id=peer, device_id_type=MESH)
    pl.semaphore_wait(barrier, len(peers))


def exchange_kernel(extent, number, *refs):
    values = refs[:number]
    outs = refs[number:2 * number]
    send_sem, recv_sem, own_sem = refs[2 * number:]
    row, col = lax.axis_index("rows"), lax.axis_index("cols")
    barrier = pltpu.get_barrier_semaphore()
    sides = [(row < extent - 1, row + 1), (row > 0, row - 1)]
    for there, other in sides:
        @pl.when(there)
        def _():
            pl.semaphore_signal(barrier, inc=1, device_id=(other, col), device_id_type=MESH)
    before = jnp.where(row > 0, 1, 0)
    after = jnp.where(row < extent - 1, 1, 0)
    pl.semaphore_wait(barrier, before + after)

    def part(i, place):
        blocks = values[i].shape[0]
        return outs[i].at[place * blocks:(place + 1) * blocks]

    def copies(way, other):
        for i in range(number):
            blocks = values[i].shape[0]
            step = -(-blocks // CHUNKS)
            for k, first in enumerate(range(0, blocks, step)):
                last = min(blocks, first + step)
                at = (2 * i + way) * CHUNKS + k
                yield pltpu.make_async_remote_copy(
                    src_ref=values[i].at[first:last],
                    dst_ref=outs[i].at[2 * way * blocks + first:2 * way * blocks + last],
                    send_sem=send_sem.at[at], recv_sem=recv_sem.at[at],
                    device_id=(other, col), device_id_type=MESH)

    for way, (there, other) in enumerate(sides):
        @pl.when(there)
        def _():
            for copy in copies(way, other):
                copy.start()
    own = [pltpu.make_async_copy(values[i], part(i, 1), own_sem.at[i]) for i in range(number)]
    for copying in own:
        copying.start()
    for way, (there, other) in enumerate(sides):
        source_there, source = sides[1 - way]

        @pl.when(source_there)
        def _():
            for copy in copies(way, source):
                copy.wait_recv()

        @pl.when(jnp.logical_not(source_there))
        def _():
            for i in range(number):
                part(i, 2 * way)[...] = jnp.zeros(values[i].shape, values[i].dtype)
    for way, (there, other) in enumerate(sides):
        @pl.when(there)
        def _():
            for copy in copies(way, other):
                copy.wait_send()
    for copying in own:
        copying.wait()


def exchange(extent, values, specs, collective_id, name):
    number = len(values)
    return pl.pallas_call(
        functools.partial(exchange_kernel, extent, number),
        out_shape=[jax.ShapeDtypeStruct((3 * v.shape[0],) + v.shape[1:], v.dtype)
                   for v in values],
        in_specs=specs,
        out_specs=[VMEM] * number,
        scratch_shapes=[pltpu.SemaphoreType.DMA((2 * number * CHUNKS,)),
                        pltpu.SemaphoreType.DMA((2 * number * CHUNKS,)),
                        pltpu.SemaphoreType.DMA((number,))],
        compiler_params=params(collective_id=collective_id, has_side_effects=True),
        cost_estimate=pl.CostEstimate(flops=0, transcendentals=0, bytes_accessed=16 << 20),
        name=name,
    )(*values)


def spread_out(extent, here, at, sources, lands, send_sem, recv_sem):
    copies = []
    for gap in range(1, extent):
        peer = lax.rem(here + gap, extent)
        copies.append(pltpu.make_async_remote_copy(
            src_ref=sources(peer), dst_ref=lands(here), send_sem=send_sem.at[gap - 1],
            recv_sem=recv_sem.at[gap - 1], device_id=at(peer), device_id_type=MESH))
        copies[-1].start()
    for copy in copies:
        copy.wait()


def gram_kernel(row_extent, col_extent, flat, gram_out, turned_out, send, turned, part, part_got,
                block, block_got, whole, last, *sems):
    row, col = lax.axis_index("rows"), lax.axis_index("cols")
    count, points = flat.shape
    piece = points // col_extent
    columns = count * col_extent

    def along_cols(peer):
        return (row, peer)

    def along_rows(peer):
        return (peer, col)

    greet(pltpu.get_barrier_semaphore(),
          [along_cols(lax.rem(col + gap, col_extent)) for gap in range(1, col_extent)]
          + [along_rows(lax.rem(row + gap, row_extent)) for gap in range(1, row_extent)])
    for peer in range(col_extent):
        send[peer] = flat[:, peer * piece:(peer + 1) * piece]
    spread_out(col_extent, col, along_cols, lambda peer: send.at[peer],
               lambda me: turned.at[me], sems[0], sems[1])
    turned[col] = send[col]
    vecs = turned[...].reshape(columns, piece)
    turned_out[...] = vecs
    part[...] = lax.dot_general(
        vecs, vecs, NT, precision=highest, preferred_element_type=F32
    ).reshape(part.shape)
    spread_out(col_extent, col, along_cols, lambda peer: part.at[peer],
               lambda me: part_got.at[me], sems[2], sems[3])
    part_got[col] = part[col]
    block[...] = sum(part_got[peer] for peer in range(col_extent))
    spread_out(row_extent, row, along_rows, lambda peer: block,
               lambda me: block_got.at[me], sems[4], sems[5])
    block_got[row] = block[...]
    last[...] = sum(block_got[peer] for peer in range(row_extent)) / (points * row_extent)
    spread_out(col_extent, col, along_cols, lambda peer: last,
               lambda me: whole.at[me], sems[6], sems[7])
    whole[col] = last[...]
    gram_out[...] = whole[...].reshape(columns, columns)


def inverse_factor(matrix):
    side = matrix.shape[0]
    count = side // 8
    shape = (8, side)
    lane = lax.broadcasted_iota(jnp.int32, shape, 1)
    sub = lax.broadcasted_iota(jnp.int32, shape, 0)
    left = [matrix[8 * g:8 * g + 8] for g in range(count)]
    right = [jnp.where(lane == sub + 8 * g, 1.0, 0.0) for g in range(count)]

    def spread_column(value, j):
        return jnp.broadcast_to(value[:, j:j + 1], shape)

    def spread_row(value, i):
        return jnp.broadcast_to(value[i:i + 1], shape)

    out = []
    for g in range(count):
        first = 8 * g
        column = [spread_column(left[g], first + k) for k in range(8)]
        entry = {(i, k): spread_row(column[k], i) for k in range(8) for i in range(k, 8)}
        inv, mult = [], {}
        for k in range(8):
            inv.append(1.0 / entry[k, k])
            for i in range(k + 1, 8):
                mult[i, k] = entry[i, k] * inv[k]
            for l in range(k + 1, 8):
                for i in range(l, 8):
                    entry[i, l] = entry[i, l] - mult[i, k] * entry[l, k]
        rows = []
        for i in range(8):
            a, w = spread_row(left[g], i), spread_row(right[g], i)
            for k in range(i):
                a = a - mult[i, k] * rows[k][0]
                w = w - mult[i, k] * rows[k][1]
            rows.append((a, w))
        done = jnp.zeros(shape, F32)
        for i in range(8):
            done = jnp.where(sub == i, rows[i][1] * (1.0 / jnp.sqrt(entry[i, i])), done)
        out.append(done)
        solved = [None] * 8
        for i in reversed(range(8)):
            a, w = rows[i][0] * inv[i], rows[i][1] * inv[i]
            for k in range(i + 1, 8):
                a = a - mult[k, i] * solved[k][0]
                w = w - mult[k, i] * solved[k][1]
            solved[i] = (a, w)
        for h in range(g + 1, count):
            a, w = left[h], right[h]
            for k in range(8):
                factor = spread_column(left[h], first + k)
                a = a - factor * solved[k][0]
                w = w - factor * solved[k][1]
            left[h], right[h] = a, w
    return jnp.concatenate(out, axis=0)


def basis_kernel(gram, turned, basis):
    inverse = inverse_factor(gram[...])
    basis[...] = jnp.dot(
        inverse, turned[...], precision=highest, preferred_element_type=F32
    ).reshape(basis.shape)


def return_kernel(col_extent, basis, out, land, send_sem, recv_sem):
    row, col = lax.axis_index("rows"), lax.axis_index("cols")
    piece = basis.shape[-1]

    def along_cols(peer):
        return (row, peer)

    greet(pltpu.get_barrier_semaphore(),
          [along_cols(lax.rem(col + gap, col_extent)) for gap in range(1, col_extent)])
    spread_out(col_extent, col, along_cols, lambda peer: basis.at[peer],
               lambda me: land.at[me], send_sem, recv_sem)
    land[col] = basis[col]
    for peer in range(col_extent):
        out[:, peer * piece:(peer + 1) * piece] = land[peer]


def held(value):
    return pltpu.with_memory_space_constraint(value, pltpu.HBM)


def params(**others):
    return pltpu.CompilerParams(vmem_limit_bytes=12 << 20, **others)


def local(row_extent, col_extent, embeddings, length_scale, start_vectors, neighbour_ids,
          neighbour_counts):
    blocks, slots = neighbour_ids.shape
    points, width = embeddings.shape
    size = points // blocks
    count = start_vectors.shape[0]
    shape = jax.ShapeDtypeStruct
    dma = pltpu.SemaphoreType.DMA
    emb = embeddings.reshape(blocks, size, width)
    spread = length_scale.astype(F32).reshape(blocks, 1, size)
    band_emb, band_spread = exchange(row_extent, (held(emb), spread), [HBM, VMEM], 0, "points_exchange")
    most = blocks * slots + GROUP
    block_f32 = shape((blocks, count, size), F32)
    block_both = shape((blocks, 2 * count, size), BF16)
    tiles, scale, panel, weighted, rows, cols, groups = pl.pallas_call(
        tiles_kernel,
        out_shape=[pltpu.VMEM((most, 2 * size, size), BF16), shape((blocks, 1, size), F32),
                   block_f32, block_both, shape((most,), jnp.int32), shape((most,), jnp.int32),
                   shape((1,), jnp.int32)],
        in_specs=[HBM] * 2 + [VMEM] * 2 + [HBM],
        out_specs=[VMEM] * 4 + [SMEM] * 3,
        scratch_shapes=[
            pltpu.VMEM((3 * blocks, size, 2 * width), BF16),
            pltpu.VMEM((3 * blocks, size, 128), F32),
            pltpu.VMEM((blocks, size, 2 * width), BF16),
            pltpu.VMEM((blocks, 1, size), F32),
            pltpu.VMEM((blocks, 1, size), F32),
            pltpu.SMEM((blocks, slots), jnp.int32),
            pltpu.SMEM((blocks,), jnp.int32),
            pltpu.VMEM((count, points), F32),
            dma((3,)),
        ],
        compiler_params=params(),
        name="tiles",
    )(held(neighbour_ids), held(neighbour_counts), band_emb, band_spread, held(start_vectors))

    for iteration in range(ITERS):
        final = iteration == ITERS - 1
        (vectors,) = exchange(row_extent, (weighted,), [VMEM], 1, "vectors_exchange")
        done = pl.pallas_call(
            functools.partial(product_kernel, final),
            out_shape=[shape((count, points), F32)] if final else [block_f32, block_both],
            in_specs=[SMEM] * 3 + [VMEM] * 4,
            out_specs=[VMEM] if final else [VMEM] * 2,
            scratch_shapes=[pltpu.VMEM((blocks, count, size), F32)],
            compiler_params=params(),
            name="product",
        )(rows, cols, groups, tiles, vectors, scale, panel)
        if final:
            flat = done[0]
        else:
            panel, weighted = done

    columns = count * col_extent
    piece = points // col_extent
    pieces = pltpu.VMEM((col_extent, count, piece), F32)
    part = pltpu.VMEM((col_extent, count, columns), F32)
    gram, turned = pl.pallas_call(
        functools.partial(gram_kernel, row_extent, col_extent),
        out_shape=[shape((columns, columns), F32), shape((columns, piece), F32)],
        in_specs=[VMEM],
        out_specs=[VMEM] * 2,
        scratch_shapes=[pieces, pieces, part, part, pltpu.VMEM((count, columns), F32),
                        pltpu.VMEM((row_extent, count, columns), F32), part,
                        pltpu.VMEM((count, columns), F32)]
        + [dma((extent - 1,)) for extent in (col_extent, col_extent, row_extent, col_extent)
           for _ in range(2)],
        compiler_params=params(collective_id=2, has_side_effects=True),
        name="gram",
    )(flat)
    basis = pl.pallas_call(
        basis_kernel,
        out_shape=shape((col_extent, count, piece), F32),
        in_specs=[VMEM] * 2,
        out_specs=VMEM,
        compiler_params=params(),
        name="basis",
    )(gram, turned)
    return pl.pallas_call(
        functools.partial(return_kernel, col_extent),
        out_shape=shape((count, points), F32),
        in_specs=[VMEM],
        out_specs=VMEM,
        scratch_shapes=[pieces, dma((col_extent - 1,)), dma((col_extent - 1,))],
        compiler_params=params(collective_id=3, has_side_effects=True),
        name="basis_return",
    )(basis)


def solution(mesh):
    placed = (P("rows", None), P("rows"), P("cols", "rows"), P("rows", None), P("rows"))
    body = functools.partial(local, mesh.shape["rows"], mesh.shape["cols"])
    return jax.shard_map(
        body, mesh=mesh, in_specs=placed, out_specs=P("cols", "rows"), check_vma=False
    )
```

```python
import functools

import jax
import jax.numpy as jnp
from jax import lax
from jax.experimental import pallas as pl
from jax.experimental.pallas import tpu as pltpu
from jax.sharding import PartitionSpec as P

ITERS = 3
GROUP = 8
CHUNKS = 3
F32 = jnp.float32
BF16 = jnp.bfloat16
highest = lax.Precision.HIGHEST
MESH = pl.DeviceIdType.MESH
VMEM = pl.BlockSpec(memory_space=pltpu.VMEM)
SMEM = pl.BlockSpec(memory_space=pltpu.SMEM)
HBM = pl.BlockSpec(memory_space=pltpu.HBM)
NT = (((1,), (1,)), ((), ()))


def split(value):
    high = value.astype(BF16)
    return high, (value - high.astype(F32)).astype(BF16)


def features(emb, left_side):
    size, width = emb.shape
    wide = emb.astype(F32)
    norm = jnp.sum(wide * wide, axis=1, keepdims=True)
    part0 = norm.astype(BF16).astype(F32)
    part1 = (norm - part0).astype(BF16).astype(F32)
    part2 = norm - part0 - part1
    lane = lax.broadcasted_iota(jnp.int32, (size, width), 1)
    base = 3 if left_side else 0
    ones = jnp.where((lane >= 3 - base) & (lane < 6 - base), 1.0, 0.0)
    side = jnp.where(lane == base, -part0, ones)
    side = jnp.where(lane == base + 1, -part1, side)
    side = jnp.where(lane == base + 2, -part2, side)
    main = wide if left_side else 2.0 * wide
    return jnp.concatenate([main.astype(BF16), side.astype(BF16)], axis=1)


def rate_of(spread, width):
    return (1.4426950408889634 / (2.0 * width)) ** 0.5 / spread


def listing(ids, counts, row_here, rows, cols):
    blocks, slots = ids.shape
    first = (row_here - 1) * blocks
    for b in range(blocks):
        rows[b] = b
        cols[b] = blocks + b
    total = jnp.int32(blocks)
    for b in range(blocks):
        count = counts[b]
        for s in range(1, slots):
            rows[total] = b
            cols[total] = ids[b, s] - first
            total = total + jnp.where(s < count, 1, 0)
    for pad in range(GROUP):
        rows[total + pad] = 0
        cols[total + pad] = blocks
    return total


def tiles_kernel(ids_there, counts_there, emb, spread, start_there,
                 tiles, scale, panel, weighted, rows, cols, groups, left, left_rate, right,
                 right_rate, degree, ids, counts, start, sem):
    band, size, width = emb.shape
    blocks = band // 3
    copies = [
        pltpu.make_async_copy(source, target, sem.at[i])
        for i, (source, target) in enumerate(
            [(ids_there, ids), (counts_there, counts), (start_there, start)])
    ]
    for copy in copies:
        copy.start()
    copies[0].wait()
    copies[1].wait()
    total = listing(ids, counts, lax.axis_index("rows"), rows, cols)
    groups[0] = (total + GROUP - 1) // GROUP
    for c in range(band):
        left[c] = features(emb[c], True)
        left_rate[c] = jnp.broadcast_to(rate_of(spread[c], width), (128, size)).T
    for b in range(blocks):
        right[b] = features(emb[blocks + b], False)
        right_rate[b] = rate_of(spread[blocks + b], width)

    def tile_of(b, c):
        gap = lax.dot_general(left[c], right[b], NT, preferred_element_type=F32)
        rate = jnp.concatenate([left_rate[c]] * (size // 128), axis=1)
        return jnp.exp2(gap * rate * right_rate[b])

    def keep(t, tile):
        high, low = split(tile)
        tiles[t, :size] = high
        tiles[t, size:] = low
        return jnp.sum(tile, axis=0, keepdims=True)

    apart = lax.broadcasted_iota(jnp.int32, (size, size), 0) != lax.broadcasted_iota(
        jnp.int32, (size, size), 1
    )
    for b in range(blocks):
        degree[b] = keep(b, jnp.where(apart, tile_of(b, blocks + b), 0.0))

    def turn(step, carry):
        first = blocks + GROUP * step
        found = []
        for t in [first + place for place in range(GROUP)]:
            b = rows[t]
            part = keep(t, tile_of(b, cols[t]))
            found.append((b, jnp.where(t < total, part, 0.0)))
        for b, part in found:
            degree[b] += part
        return carry

    lax.fori_loop(0, (total - blocks + GROUP - 1) // GROUP, turn, 0)
    for pad in range(GROUP - 1):
        tiles[total + pad] = jnp.zeros((2 * size, size), BF16)
    copies[2].wait()
    count = start.shape[0]
    for b in range(blocks):
        factor = 1.0 / jnp.sqrt(degree[b])
        scale[b] = factor
        vecs = start[:, b * size:(b + 1) * size]
        panel[b] = vecs
        high, low = split(vecs * factor)
        weighted[b, :count] = high
        weighted[b, count:] = low


def product_kernel(final, rows, cols, groups, tiles, vectors, scale, panel, *rest):
    if final:
        out, total = rest
    else:
        out, weighted, total = rest
    blocks, count, size = panel.shape
    total[...] = jnp.zeros(total.shape, F32)

    def one(group, carry):
        found = []
        for place in range(GROUP):
            t = group * GROUP + place
            both = vectors[cols[t]]
            value = jnp.dot(both, tiles[t, :size], preferred_element_type=F32)
            more = jnp.dot(both[:count], tiles[t, size:], preferred_element_type=F32)
            found.append((rows[t], value[:count] + value[count:] + more))
        for b, value in found:
            total[b] += value
        return carry

    lax.fori_loop(0, groups[0], one, 0)
    for b in range(blocks):
        factor = scale[b]
        vecs = 0.5 * (panel[b] + factor * total[b])
        if final:
            out[:, b * size:(b + 1) * size] = vecs
        else:
            out[b] = vecs
            high, low = split(vecs * factor)
            weighted[b, :count] = high
            weighted[b, count:] = low


def greet(barrier, peers):
    for peer in peers:
        pl.semaphore_signal(barrier, inc=1, device_id=peer, device_id_type=MESH)
    pl.semaphore_wait(barrier, len(peers))


def exchange_kernel(extent, number, *refs):
    values = refs[:number]
    outs = refs[number:2 * number]
    send_sem, recv_sem, own_sem = refs[2 * number:]
    row, col = lax.axis_index("rows"), lax.axis_index("cols")
    barrier = pltpu.get_barrier_semaphore()
    sides = [(row < extent - 1, row + 1), (row > 0, row - 1)]
    for there, other in sides:
        @pl.when(there)
        def _():
            pl.semaphore_signal(barrier, inc=1, device_id=(other, col), device_id_type=MESH)
    before = jnp.where(row > 0, 1, 0)
    after = jnp.where(row < extent - 1, 1, 0)
    pl.semaphore_wait(barrier, before + after)

    def part(i, place):
        blocks = values[i].shape[0]
        return outs[i].at[place * blocks:(place + 1) * blocks]

    def copies(way, other):
        for i in range(number):
            blocks = values[i].shape[0]
            step = -(-blocks // CHUNKS)
            for k, first in enumerate(range(0, blocks, step)):
                last = min(blocks, first + step)
                at = (2 * i + way) * CHUNKS + k
                yield pltpu.make_async_remote_copy(
                    src_ref=values[i].at[first:last],
                    dst_ref=outs[i].at[2 * way * blocks + first:2 * way * blocks + last],
                    send_sem=send_sem.at[at], recv_sem=recv_sem.at[at],
                    device_id=(other, col), device_id_type=MESH)

    for way, (there, other) in enumerate(sides):
        @pl.when(there)
        def _():
            for copy in copies(way, other):
                copy.start()
    own = [pltpu.make_async_copy(values[i], part(i, 1), own_sem.at[i]) for i in range(number)]
    for copying in own:
        copying.start()
    for way, (there, other) in enumerate(sides):
        source_there, source = sides[1 - way]

        @pl.when(source_there)
        def _():
            for copy in copies(way, source):
                copy.wait_recv()

        @pl.when(jnp.logical_not(source_there))
        def _():
            for i in range(number):
                part(i, 2 * way)[...] = jnp.zeros(values[i].shape, values[i].dtype)
    for way, (there, other) in enumerate(sides):
        @pl.when(there)
        def _():
            for copy in copies(way, other):
                copy.wait_send()
    for copying in own:
        copying.wait()


def exchange(extent, values, specs, collective_id, name):
    number = len(values)
    return pl.pallas_call(
        functools.partial(exchange_kernel, extent, number),
        out_shape=[jax.ShapeDtypeStruct((3 * v.shape[0],) + v.shape[1:], v.dtype)
                   for v in values],
        in_specs=specs,
        out_specs=[VMEM] * number,
        scratch_shapes=[pltpu.SemaphoreType.DMA((2 * number * CHUNKS,)),
                        pltpu.SemaphoreType.DMA((2 * number * CHUNKS,)),
                        pltpu.SemaphoreType.DMA((number,))],
        compiler_params=params(collective_id=collective_id, has_side_effects=True),
        cost_estimate=pl.CostEstimate(flops=0, transcendentals=0, bytes_accessed=16 << 20),
        name=name,
    )(*values)


def spread_out(extent, here, at, sources, lands, send_sem, recv_sem):
    copies = []
    for gap in range(1, extent):
        peer = lax.rem(here + gap, extent)
        copies.append(pltpu.make_async_remote_copy(
            src_ref=sources(peer), dst_ref=lands(here), send_sem=send_sem.at[gap - 1],
            recv_sem=recv_sem.at[gap - 1], device_id=at(peer), device_id_type=MESH))
        copies[-1].start()
    for copy in copies:
        copy.wait()


def gram_kernel(row_extent, col_extent, flat, gram_out, turned_out, send, turned, part, part_got,
                block, block_got, whole, last, *sems):
    row, col = lax.axis_index("rows"), lax.axis_index("cols")
    count, points = flat.shape
    piece = points // col_extent
    columns = count * col_extent

    def along_cols(peer):
        return (row, peer)

    def along_rows(peer):
        return (peer, col)

    greet(pltpu.get_barrier_semaphore(),
          [along_cols(lax.rem(col + gap, col_extent)) for gap in range(1, col_extent)]
          + [along_rows(lax.rem(row + gap, row_extent)) for gap in range(1, row_extent)])
    for peer in range(col_extent):
        send[peer] = flat[:, peer * piece:(peer + 1) * piece]
    spread_out(col_extent, col, along_cols, lambda peer: send.at[peer],
               lambda me: turned.at[me], sems[0], sems[1])
    turned[col] = send[col]
    vecs = turned[...].reshape(columns, piece)
    turned_out[...] = vecs
    part[...] = lax.dot_general(
        vecs, vecs, NT, precision=highest, preferred_element_type=F32
    ).reshape(part.shape)
    spread_out(col_extent, col, along_cols, lambda peer: part.at[peer],
               lambda me: part_got.at[me], sems[2], sems[3])
    part_got[col] = part[col]
    block[...] = sum(part_got[peer] for peer in range(col_extent))
    spread_out(row_extent, row, along_rows, lambda peer: block,
               lambda me: block_got.at[me], sems[4], sems[5])
    block_got[row] = block[...]
    last[...] = sum(block_got[peer] for peer in range(row_extent)) / (points * row_extent)
    spread_out(col_extent, col, along_cols, lambda peer: last,
               lambda me: whole.at[me], sems[6], sems[7])
    whole[col] = last[...]
    gram_out[...] = whole[...].reshape(columns, columns)


def inverse_factor(matrix):
    side = matrix.shape[0]
    count = side // 8
    shape = (8, side)
    lane = lax.broadcasted_iota(jnp.int32, shape, 1)
    sub = lax.broadcasted_iota(jnp.int32, shape, 0)
    left = [matrix[8 * g:8 * g + 8] for g in range(count)]
    right = [jnp.where(lane == sub + 8 * g, 1.0, 0.0) for g in range(count)]

    def spread_column(value, j):
        return jnp.broadcast_to(value[:, j:j + 1], shape)

    def spread_row(value, i):
        return jnp.broadcast_to(value[i:i + 1], shape)

    out = []
    for g in range(count):
        first = 8 * g
        column = [spread_column(left[g], first + k) for k in range(8)]
        entry = {(i, k): spread_row(column[k], i) for k in range(8) for i in range(k, 8)}
        inv, mult = [], {}
        for k in range(8):
            inv.append(1.0 / entry[k, k])
            for i in range(k + 1, 8):
                mult[i, k] = entry[i, k] * inv[k]
            for l in range(k + 1, 8):
                for i in range(l, 8):
                    entry[i, l] = entry[i, l] - mult[i, k] * entry[l, k]
        rows = []
        for i in range(8):
            a, w = spread_row(left[g], i), spread_row(right[g], i)
            for k in range(i):
                a = a - mult[i, k] * rows[k][0]
                w = w - mult[i, k] * rows[k][1]
            rows.append((a, w))
        done = jnp.zeros(shape, F32)
        for i in range(8):
            done = jnp.where(sub == i, rows[i][1] * (1.0 / jnp.sqrt(entry[i, i])), done)
        out.append(done)
        solved = [None] * 8
        for i in reversed(range(8)):
            a, w = rows[i][0] * inv[i], rows[i][1] * inv[i]
            for k in range(i + 1, 8):
                a = a - mult[k, i] * solved[k][0]
                w = w - mult[k, i] * solved[k][1]
            solved[i] = (a, w)
        for h in range(g + 1, count):
            a, w = left[h], right[h]
            for k in range(8):
                factor = spread_column(left[h], first + k)
                a = a - factor * solved[k][0]
                w = w - factor * solved[k][1]
            left[h], right[h] = a, w
    return jnp.concatenate(out, axis=0)


def basis_kernel(gram, turned, basis):
    inverse = inverse_factor(gram[...])
    basis[...] = jnp.dot(
        inverse, turned[...], precision=highest, preferred_element_type=F32
    ).reshape(basis.shape)


def return_kernel(col_extent, basis, out, land, send_sem, recv_sem):
    row, col = lax.axis_index("rows"), lax.axis_index("cols")
    piece = basis.shape[-1]

    def along_cols(peer):
        return (row, peer)

    greet(pltpu.get_barrier_semaphore(),
          [along_cols(lax.rem(col + gap, col_extent)) for gap in range(1, col_extent)])
    spread_out(col_extent, col, along_cols, lambda peer: basis.at[peer],
               lambda me: land.at[me], send_sem, recv_sem)
    land[col] = basis[col]
    for peer in range(col_extent):
        out[:, peer * piece:(peer + 1) * piece] = land[peer]


def held(value):
    return pltpu.with_memory_space_constraint(value, pltpu.HBM)


def params(**others):
    return pltpu.CompilerParams(vmem_limit_bytes=12 << 20, **others)


def local(row_extent, col_extent, embeddings, length_scale, start_vectors, neighbour_ids,
          neighbour_counts):
    blocks, slots = neighbour_ids.shape
    points, width = embeddings.shape
    size = points // blocks
    count = start_vectors.shape[0]
    shape = jax.ShapeDtypeStruct
    dma = pltpu.SemaphoreType.DMA
    emb = embeddings.reshape(blocks, size, width)
    spread = length_scale.astype(F32).reshape(blocks, 1, size)
    band_emb, band_spread = exchange(row_extent, (held(emb), spread), [HBM, VMEM], 0, "points_exchange")
    most = blocks * slots + GROUP
    block_f32 = shape((blocks, count, size), F32)
    block_both = shape((blocks, 2 * count, size), BF16)
    tiles, scale, panel, weighted, rows, cols, groups = pl.pallas_call(
        tiles_kernel,
        out_shape=[pltpu.VMEM((most, 2 * size, size), BF16), shape((blocks, 1, size), F32),
                   block_f32, block_both, shape((most,), jnp.int32), shape((most,), jnp.int32),
                   shape((1,), jnp.int32)],
        in_specs=[HBM] * 2 + [VMEM] * 2 + [HBM],
        out_specs=[VMEM] * 4 + [SMEM] * 3,
        scratch_shapes=[
            pltpu.VMEM((3 * blocks, size, 2 * width), BF16),
            pltpu.VMEM((3 * blocks, size, 128), F32),
            pltpu.VMEM((blocks, size, 2 * width), BF16),
            pltpu.VMEM((blocks, 1, size), F32),
            pltpu.VMEM((blocks, 1, size), F32),
            pltpu.SMEM((blocks, slots), jnp.int32),
            pltpu.SMEM((blocks,), jnp.int32),
            pltpu.VMEM((count, points), F32),
            dma((3,)),
        ],
        compiler_params=params(),
        name="tiles",
    )(held(neighbour_ids), held(neighbour_counts), band_emb, band_spread, held(start_vectors))

    for iteration in range(ITERS):
        final = iteration == ITERS - 1
        (vectors,) = exchange(row_extent, (weighted,), [VMEM], 1, "vectors_exchange")
        done = pl.pallas_call(
            functools.partial(product_kernel, final),
            out_shape=[shape((count, points), F32)] if final else [block_f32, block_both],
            in_specs=[SMEM] * 3 + [VMEM] * 4,
            out_specs=[VMEM] if final else [VMEM] * 2,
            scratch_shapes=[pltpu.VMEM((blocks, count, size), F32)],
            compiler_params=params(),
            name="product",
        )(rows, cols, groups, tiles, vectors, scale, panel)
        if final:
            flat = done[0]
        else:
            panel, weighted = done

    columns = count * col_extent
    piece = points // col_extent
    pieces = pltpu.VMEM((col_extent, count, piece), F32)
    part = pltpu.VMEM((col_extent, count, columns), F32)
    gram, turned = pl.pallas_call(
        functools.partial(gram_kernel, row_extent, col_extent),
        out_shape=[shape((columns, columns), F32), shape((columns, piece), F32)],
        in_specs=[VMEM],
        out_specs=[VMEM] * 2,
        scratch_shapes=[pieces, pieces, part, part, pltpu.VMEM((count, columns), F32),
                        pltpu.VMEM((row_extent, count, columns), F32), part,
                        pltpu.VMEM((count, columns), F32)]
        + [dma((extent - 1,)) for extent in (col_extent, col_extent, row_extent, col_extent)
           for _ in range(2)],
        compiler_params=params(collective_id=2, has_side_effects=True),
        name="gram",
    )(flat)
    basis = pl.pallas_call(
        basis_kernel,
        out_shape=shape((col_extent, count, piece), F32),
        in_specs=[VMEM] * 2,
        out_specs=VMEM,
        compiler_params=params(),
        name="basis",
    )(gram, turned)
    return pl.pallas_call(
        functools.partial(return_kernel, col_extent),
        out_shape=shape((count, points), F32),
        in_specs=[VMEM],
        out_specs=VMEM,
        scratch_shapes=[pieces, dma((col_extent - 1,)), dma((col_extent - 1,))],
        compiler_params=params(collective_id=3, has_side_effects=True),
        name="basis_return",
    )(basis)


def solution(mesh):
    placed = (P("rows", None), P("rows"), P("cols", "rows"), P("rows", None), P("rows"))
    body = functools.partial(local, mesh.shape["rows"], mesh.shape["cols"])
    return jax.shard_map(
        body, mesh=mesh, in_specs=placed, out_specs=P("cols", "rows"), check_vma=False
    )
```
